32 devices in a mesh: wide: 8 (over z, x), narrow: 4 (over y, core).
Axes of the slice: x: 2, y: 2, z: 4, core: 2. Of those that a mesh axis runs over, the one named last changes fastest.
Arguments:
- hidden: bfloat16 [512, 4096], P('narrow', 'wide'), may hold values from -6 to 6
- attn_gain: float32 [4096], replicated, may hold values from 0.5 to 1.5
- query_weight: bfloat16 [4096, 4096], P(None, 'wide'), may hold values from -0.09375 to 0.09375
- key_weight: bfloat16 [4096, 1024], P('wide'), may hold values from -0.125 to 0.125
- value_weight: bfloat16 [4096, 1024], P('wide'), may hold values from -0.125 to 0.125
- out_weight: bfloat16 [4096, 4096], P('wide'), may hold values from -0.09375 to 0.09375
- cache_key: bfloat16 [8, 512, 128], replicated, may hold values from -600 to 600
- cache_value: bfloat16 [8, 512, 128], replicated, may hold values from -6 to 6
- mlp_gain: float32 [4096], replicated, may hold values from 0.5 to 1.5
- router_weight: bfloat16 [4096, 16], replicated, may hold values from -0.09375 to 0.09375
- expert_ids: int32 [512, 2], P('narrow'), may hold values from 0 to 15, all different within a row; in each aligned block of 16 rows (0 to 15, 16 to 31, ...) at most 4 rows name the same one
- gate_weight: bfloat16 [32, 4096, 3200], P('wide', None, 'narrow'), may hold values from -0.09375 to 0.09375
- up_weight: bfloat16 [32, 4096, 3200], P('wide', None, 'narrow'), may hold values from -0.09375 to 0.09375
- down_weight: bfloat16 [32, 3200, 4096], P('wide', 'narrow'), may hold values from -0.078125 to 0.078125
Outputs:
- layer_out: bfloat16 [512, 4096], P('narrow', 'wide')
The draws below stay inside these ranges and needn't reach their ends.
Inputs may be any that keep to these rules, and one draw needn't show every extreme that they name: `expert_ids`: in each aligned block of 16 rows no expert is named by more than 4 rows, and in every block some expert by exactly 4; the two experts of a row differ.
All inputs are finite; a program needn't handle non-finite values.
Results may differ from the reference program's by a relative error of at most 0.012.
The reference program's roundings to bfloat16 on the way count: a program that leaves them out, or rounds other values in their place, can miss the bound.
Values may be sent and summed in bfloat16 or wider, within the bound.
No kernel may reach another device: no remote copies, remote signals or barrier semaphores. Data moves between devices by JAX's collectives and lax.ppermute only.
A program may use at most 192 MiB of HBM per device.

```python
import math
import jax
import jax.numpy as jnp
import numpy as np
from jax import lax

D = 4096
HEADS = 32
KV_HEADS = 8
HEAD_DIM = 128
FF = 6400
EXPERTS = 16
SPLIT = 2
TOK_BLOCK = 16
CTX = 512
SPAN = 512
CAPD = 4
SLOTS = 32


def draw_cache_key(key, part):
    base = jax.random.normal(key, (KV_HEADS, CTX, HEAD_DIM), jnp.float32)
    return jnp.clip(base, -600.0, 600.0).astype(jnp.bfloat16)


def with_spikes(array, stream_key, source, target, blocks, factor):
    owner, partner = [(jnp.arange(array.shape[dim]) // (array.shape[dim] // blocks)).reshape([-1 if axis == dim else 1 for axis in range(array.ndim)]) for dim in (source, target)]
    chosen = jax.random.permutation(stream_key, blocks)[partner]
    strong = (owner == chosen) | (owner == (partner + blocks // 2) % blocks)
    return jnp.where(strong, factor * array, array)


def level_of(key, dims, cuts, low, high):
    def one(axis_at, shards_of):
        heights = jax.random.uniform(jax.random.fold_in(jax.random.fold_in(key, 6), axis_at), (shards_of,), jnp.float32, low / len(cuts), high / len(cuts))
        return jnp.repeat(jnp.exp(heights), dims[axis_at] // shards_of).reshape((-1,) + (1,) * (len(dims) - axis_at - 1))

    level = one(*cuts[0])
    for cut in cuts[1:]:
        level = level * one(*cut)
    return level


def deal_out(own_key, own, number, rows, count, top, reach, slope):
    sequence = jax.random.permutation(own_key, count)
    heavy_load, common = shares(count, rows * top, reach, slope, True), shares(count, rows * top, reach, slope, False)
    places = jnp.arange(count)

    def named(lengths, offset_by):
        used = int((lengths > 0).sum())
        fixed = max(1, used // 4)
        shifted = fixed + (places - fixed + offset_by * (used - fixed)) % max(1, count - fixed)
        return jnp.zeros((count,), jnp.int32).at[sequence[jnp.where(places < fixed, places, shifted)]].set(jnp.asarray(lengths, jnp.int32))

    lengths = jnp.where(number % 4 == 0, named(heavy_load, number // 4), named(common, number - number // 4 - 1))
    mixed = jax.random.permutation(jax.random.fold_in(own, 3), count)
    source_of, sink = mixed[0:count // 2 * 2:2], mixed[1:count // 2 * 2:2]
    slack = jnp.minimum(lengths[source_of] - 1, reach - lengths[sink]) // 2
    slack = jnp.where((source_of == sequence[0]) | (sink == sequence[0]) | (lengths[sink] == 0), 0, jnp.maximum(slack, 0))
    shifted = jax.random.randint(jax.random.fold_in(own, 4), (count // 2,), 0, 1 << 20) % (slack + 1)
    lengths = lengths.at[source_of].add(-shifted).at[sink].add(shifted)
    labels = jnp.searchsorted(jnp.cumsum(lengths), jnp.arange(rows * top), side="right").astype(jnp.int32)
    grid = labels.reshape(top, rows).T
    grid = grid[jax.random.permutation(jax.random.fold_in(own, 1), rows)]
    offset_by = jax.random.randint(jax.random.fold_in(own, 2), (rows, 1), 0, top)
    return jnp.take_along_axis(grid, (jnp.arange(top)[None, :] + offset_by) % top, axis=1)


def shares(count, total, limit, slope, full):
    weights = [(1 << 20) // math.isqrt(standing ** slope) + 1 for standing in range(1, count + 1)]
    largest = limit if full else min(limit, max(-(-total // count), total * weights[0] // sum(weights)))
    least = 1 if total - largest >= count - 1 else 0
    given, surplus = [largest] + [least] * (count - 1), total - largest - least * (count - 1)
    while surplus > 0:
        candidates = [i for i in range(1, count) if given[i] < largest] or [i for i in range(1, count) if given[i] < limit]
        mass, remaining = sum([weights[i] for i in candidates]), surplus
        for i in candidates:
            addition = min(limit - given[i], max(1, remaining * weights[i] // mass), surplus)
            given[i] = given[i] + addition
            surplus = surplus - addition
    return np.array(given)


def normal_values(rng, extent, deviation, bound, pieces=(), kind=jnp.bfloat16):
    values = jax.random.normal(rng, extent, jnp.float32) * deviation
    if len(pieces) > 0:
        values = level_of(rng, extent, pieces, -0.22, 0.18) * values
    return jnp.clip(values, min=-bound, max=bound).astype(kind)


def bell_draw_with(rng, extent, spread, limit, shards, heavy, kind=jnp.bfloat16):
    entries = spread * jax.random.normal(rng, extent, jnp.float32)
    if shards:
        entries = entries * level_of(rng, extent, shards, -0.22, 0.18)
    return jnp.clip(with_spikes(entries, jax.random.fold_in(rng, 3), *heavy), -limit, limit).astype(kind)


def setup_inputs(seed: int = 0) -> dict:
    key_of = jax.random.split(jax.random.key(seed), 15)
    hidden = normal_values(key_of[0], (SPAN, D), 1.0, 6.0, ((0, 4), (1, 8)))
    attn_gain = jnp.clip(1.0 + 0.1 * jax.random.normal(key_of[1], (D,), jnp.float32), 0.5, 1.5)
    query_weight = normal_values(key_of[2], (D, HEADS * HEAD_DIM), D ** -0.5, 0.09375, ((1, 8),))
    key_weight = bell_draw_with(key_of[3], (D, KV_HEADS * HEAD_DIM), D ** -0.5, 0.125, ((0, 8),), (0, 1, 8, 2.0))
    value_weight = bell_draw_with(key_of[4], (D, KV_HEADS * HEAD_DIM), D ** -0.5, 0.125, ((0, 8),), (0, 1, 8, 2.0))
    out_weight = normal_values(key_of[5], (HEADS * HEAD_DIM, D), (HEADS * HEAD_DIM) ** -0.5, 0.09375, ((0, 8),))
    cache_key = draw_cache_key(jax.random.fold_in(key_of[14], 71), 0)
    cache_value = normal_values(key_of[7], (KV_HEADS, CTX, HEAD_DIM), 1.0, 6.0)
    mlp_gain = jnp.clip(1.0 + 0.1 * jax.random.normal(key_of[8], (D,), jnp.float32), 0.5, 1.5)
    router_weight = normal_values(key_of[9], (D, EXPERTS), D ** -0.5, 0.09375)
    expert_ids_keys = jax.random.split(jax.random.fold_in(key_of[10], 1), SPAN // TOK_BLOCK)
    expert_ids_turns = jax.random.permutation(jax.random.fold_in(key_of[10], 3), SPAN // TOK_BLOCK)
    expert_ids = jax.vmap(lambda own, number: deal_out(jax.random.fold_in(key_of[10], 2), own, number, TOK_BLOCK, EXPERTS, 2, CAPD, 2))(expert_ids_keys, expert_ids_turns).reshape((SPAN, 2))
    gate_weight = normal_values(key_of[11], (SLOTS, D, FF // SPLIT), D ** -0.5, 0.09375, ((0, 8), (2, 4)))
    up_weight = normal_values(key_of[12], (SLOTS, D, FF // SPLIT), D ** -0.5, 0.09375, ((0, 8), (2, 4)))
    down_weight = normal_values(key_of[13], (SLOTS, FF // SPLIT, D), FF ** -0.5, 0.078125, ((0, 8), (1, 4)))
    return dict(hidden=hidden, attn_gain=attn_gain, query_weight=query_weight, key_weight=key_weight, value_weight=value_weight, out_weight=out_weight, cache_key=cache_key, cache_value=cache_value, mlp_gain=mlp_gain, router_weight=router_weight, expert_ids=expert_ids, gate_weight=gate_weight, up_weight=up_weight, down_weight=down_weight)


epsilon = 1e-05

def layer_normed(values, gain):
    average = lax.optimization_barrier(jnp.mean(values, axis=-1, keepdims=True))
    centered = values - average
    variance = lax.optimization_barrier(jnp.mean(centered * centered, axis=-1, keepdims=True))
    return centered * lax.rsqrt(variance + epsilon) * gain

def slot_targets(routing, experts, capacity):
    blocks = routing.shape[0]
    flat_ids = routing.reshape(blocks, -1)
    onehot = (flat_ids[:, :, None] == jnp.arange(experts, dtype=jnp.int32)[None, None, :]).astype(jnp.int32)
    earlier = jnp.cumsum(onehot, axis=1) - onehot
    position = lax.optimization_barrier(jnp.sum(earlier * onehot, axis=2))
    return (flat_ids * capacity + position).reshape(routing.shape)

def fill_buffer(normed, target, slot_count):
    matches = (target[:, :, :, None] == jnp.arange(slot_count, dtype=jnp.int32)).astype(jnp.float32)
    placing = lax.optimization_barrier(jnp.sum(matches, axis=2))
    return jnp.einsum('btj,btd->bjd', placing, normed.astype(jnp.float32)).astype(jnp.bfloat16)

def pair_weights(logits, routing):
    picked = jnp.take_along_axis(logits, routing, axis=-1)
    leading = jax.nn.sigmoid(picked[..., 0] - picked[..., 1])
    return jnp.stack([leading, 1.0 - leading], axis=-1)

def gather_back(results, target, weights):
    blocks, slot_count = (results.shape[0], results.shape[1])
    flat_rows = results.reshape(blocks * slot_count, results.shape[2])
    row_index = target + (jnp.arange(blocks, dtype=jnp.int32) * slot_count)[:, None, None]
    picked = jnp.take(flat_rows, row_index.reshape(-1), axis=0).reshape(target.shape + (results.shape[2],))
    return lax.optimization_barrier(jnp.sum(picked * weights[..., None], axis=2))

def reference(hidden, attn_gain, query_weight, key_weight, value_weight, out_weight, cache_key, cache_value, mlp_gain, router_weight, expert_ids, gate_weight, up_weight, down_weight):
    share = HEADS // KV_HEADS
    normed = layer_normed(hidden.astype(jnp.float32), attn_gain).astype(jnp.bfloat16)
    queries = jnp.dot(normed, query_weight, preferred_element_type=jnp.float32).astype(jnp.bfloat16)
    fresh_keys = jnp.dot(normed, key_weight, preferred_element_type=jnp.float32).astype(jnp.bfloat16)
    fresh_values = jnp.dot(normed, value_weight, preferred_element_type=jnp.float32).astype(jnp.bfloat16)
    queries = queries.reshape(SPAN, HEADS, HEAD_DIM).transpose(1, 0, 2)
    fresh_keys = jnp.repeat(fresh_keys.reshape(SPAN, KV_HEADS, HEAD_DIM).transpose(1, 0, 2), share, axis=0)
    fresh_values = jnp.repeat(fresh_values.reshape(SPAN, KV_HEADS, HEAD_DIM).transpose(1, 0, 2), share, axis=0)
    old_keys_all = jnp.repeat(cache_key, share, axis=0)
    old_values_all = jnp.repeat(cache_value, share, axis=0)
    row_ids = jnp.arange(SPAN, dtype=jnp.int32)
    key_ids = jnp.arange(CTX + SPAN, dtype=jnp.int32) - CTX
    allowed = key_ids[None, :] <= row_ids[:, None]

    def one_head(items):
        head_query, old_keys, old_values, new_keys, new_values = items
        all_keys = jnp.concatenate([old_keys, new_keys], axis=0)
        all_values = jnp.concatenate([old_values, new_values], axis=0)
        scores = jnp.dot(head_query, all_keys.T, preferred_element_type=jnp.float32) * HEAD_DIM ** (-0.5)
        scores = jnp.where(allowed, scores, -1e+30)
        highest = lax.optimization_barrier(jnp.max(scores, axis=1, keepdims=True))
        weights = jnp.exp(scores - highest)
        weights = (weights / lax.optimization_barrier(jnp.sum(weights, axis=1, keepdims=True))).astype(jnp.bfloat16)
        return jnp.dot(weights, all_values, preferred_element_type=jnp.float32).astype(jnp.bfloat16)
    attended = lax.map(one_head, (queries, old_keys_all, old_values_all, fresh_keys, fresh_values))
    attended = attended.transpose(1, 0, 2).reshape(SPAN, HEADS * HEAD_DIM)
    head_mix = jnp.dot(attended, out_weight, preferred_element_type=jnp.float32)
    residual = (hidden.astype(jnp.float32) + head_mix).astype(jnp.bfloat16)
    normed_two = layer_normed(residual.astype(jnp.float32), mlp_gain).astype(jnp.bfloat16)
    logits = jnp.dot(normed_two, router_weight, preferred_element_type=jnp.float32)
    blocks = SPAN // TOK_BLOCK
    routing = expert_ids.reshape(blocks, TOK_BLOCK, 2)
    target = slot_targets(routing, EXPERTS, CAPD)
    buffer = fill_buffer(normed_two.reshape(blocks, TOK_BLOCK, D), target, EXPERTS * CAPD)
    buffer = buffer.reshape(blocks, EXPERTS, CAPD, D)

    def one_slot(items):
        slot_index, w_gate, w_up, w_down = items
        tokens_in = jnp.take(buffer, slot_index // SPLIT, axis=1).reshape(blocks * CAPD, D)
        gate_term = jnp.dot(tokens_in, w_gate, preferred_element_type=jnp.float32)
        up_term = jnp.dot(tokens_in, w_up, preferred_element_type=jnp.float32)
        active = (jax.nn.silu(gate_term) * up_term).astype(jnp.bfloat16)
        return jnp.dot(active, w_down, preferred_element_type=jnp.float32).astype(jnp.bfloat16).reshape(blocks, CAPD, D)
    slot_out = lax.map(one_slot, (jnp.arange(EXPERTS * SPLIT, dtype=jnp.int32), gate_weight, up_weight, down_weight))
    summed = lax.optimization_barrier(jnp.sum(slot_out.reshape(EXPERTS, SPLIT, blocks, CAPD, D).astype(jnp.float32), axis=1))
    summed = summed.transpose(1, 0, 2, 3).reshape(blocks, EXPERTS * CAPD, D)
    mixture = gather_back(summed, target, pair_weights(logits.reshape(blocks, TOK_BLOCK, EXPERTS), routing))
    return (residual.astype(jnp.float32) + mixture.reshape(SPAN, D)).astype(jnp.bfloat16)
```

```python
import jax
import jax.numpy as jnp
import numpy as np
from jax import lax
from jax.sharding import PartitionSpec as P

SPLIT = 2
CAPD = 4
TOK_BLOCK = 16
DIRECT_LIMIT = 8


epsilon = 1e-05


def layer_normed(values, gain):
    average = jnp.mean(values, axis=-1, keepdims=True)
    centered = values - average
    variance = jnp.mean(centered * centered, axis=-1, keepdims=True)
    return centered * lax.rsqrt(variance + epsilon) * gain


def swap(values, axis, distance):
    count = lax.axis_size(axis)
    return lax.ppermute(values, axis, [(i, i ^ distance) for i in range(count)])


def is_power_of_two(count):
    return count & (count - 1) == 0


def gather_blocks(values, axis):
    count = lax.axis_size(axis)
    if count > DIRECT_LIMIT or not is_power_of_two(count):
        return lax.all_gather(values, axis, axis=0)
    index = lax.axis_index(axis)
    stacked = jnp.zeros((count,) + values.shape, values.dtype)
    for distance in range(count):
        block = values if distance == 0 else swap(values, axis, distance)
        stacked = lax.dynamic_update_index_in_dim(stacked, block, index ^ distance, 0)
    return stacked


def slot_targets(routing, experts, capacity):
    blocks = routing.shape[0]
    flat_ids = routing.reshape(blocks, -1)
    onehot = (flat_ids[:, :, None] == jnp.arange(experts, dtype=jnp.int32)[None, None, :]).astype(
        jnp.int32
    )
    earlier = jnp.cumsum(onehot, axis=1) - onehot
    position = jnp.sum(earlier * onehot, axis=2)
    return (flat_ids * capacity + position).reshape(routing.shape)


def attend(queries, all_keys, all_values, first_row, context):
    row_count, heads_here, head_size = queries.shape
    kv_here = all_keys.shape[0]
    grouped = queries.reshape(row_count, kv_here, heads_here // kv_here, head_size)
    scale_factor = head_size ** (-0.5)
    scores = (
        jnp.einsum("rgqd,gkd->gqrk", grouped, all_keys, preferred_element_type=jnp.float32)
        * scale_factor
    )
    row_ids = first_row + jnp.arange(row_count, dtype=jnp.int32)
    key_ids = jnp.arange(all_keys.shape[1], dtype=jnp.int32) - context
    allowed = key_ids[None, :] <= row_ids[:, None]
    scores = jnp.where(allowed[None, None], scores, -1e30)
    highest = jnp.max(scores, axis=3, keepdims=True)
    weights = jnp.exp(scores - highest)
    weights = (weights / jnp.sum(weights, axis=3, keepdims=True)).astype(jnp.bfloat16)
    mixed = jnp.einsum(
        "gqrk,gkd->rgqd", weights, all_values, preferred_element_type=jnp.float32
    ).astype(jnp.bfloat16)
    return mixed.reshape(row_count, heads_here, head_size)


def sum_over_narrow(partial):
    count = lax.axis_size("narrow")
    index = lax.axis_index("narrow")
    if not is_power_of_two(count):
        return lax.psum_scatter(partial, "narrow", scatter_dimension=0, tiled=False)
    kept = partial
    distance = 1
    while distance < count:
        grouped = kept.reshape((kept.shape[0] // 2, 2) + kept.shape[1:])
        bit = (index // distance) % 2
        own = lax.dynamic_index_in_dim(grouped, bit, 1, keepdims=False)
        other = lax.dynamic_index_in_dim(grouped, 1 - bit, 1, keepdims=False)
        arrived = swap(other.astype(jnp.bfloat16), "narrow", distance)
        kept = own + arrived.astype(jnp.float32)
        distance *= 2
    return kept[0]


def gather_over_narrow(rows):
    count = lax.axis_size("narrow")
    index = lax.axis_index("narrow")
    if not is_power_of_two(count):
        return lax.all_gather(rows, "narrow", axis=0)
    held = rows[None]
    distance = count // 2
    while distance >= 1:
        arrived = swap(held, "narrow", distance)
        bit = (index // distance) % 2
        low = jnp.where(bit == 0, held, arrived)
        high = jnp.where(bit == 0, arrived, held)
        held = jnp.stack([low, high], axis=0).reshape((-1,) + rows.shape)
        distance //= 2
    bits = count.bit_length() - 1
    order = [sum(((i >> b) & 1) << (bits - 1 - b) for b in range(bits)) for i in range(count)]
    return jnp.stack([held[order[i]] for i in range(count)], axis=0)


def body(
    hidden,
    attn_gain,
    query_weight,
    key_weight,
    value_weight,
    out_weight,
    cache_key,
    cache_value,
    mlp_gain,
    router_weight,
    expert_ids,
    gate_weight,
    up_weight,
    down_weight,
):
    f32, bf16 = jnp.float32, jnp.bfloat16
    wide_count = lax.axis_size("wide")
    wide_index = lax.axis_index("wide")
    narrow_count = lax.axis_size("narrow")
    narrow_index = lax.axis_index("narrow")
    row_count, feature_share = hidden.shape
    feature_count = feature_share * wide_count
    kv_total, context, head_size = cache_key.shape
    heads_here = query_weight.shape[1] // head_size
    share = heads_here * wide_count // kv_total
    kv_here = max(heads_here // share, 1)
    kv_start = wide_index * heads_here // share

    experts = router_weight.shape[1]
    slots_here = gate_weight.shape[0]
    experts_here = max(slots_here // SPLIT, 1)
    parts_here = slots_here // experts_here
    blocks = row_count // TOK_BLOCK
    routing = expert_ids.reshape(blocks, TOK_BLOCK, 2)
    target = slot_targets(routing, experts, CAPD).reshape(row_count, 2)
    token_block = np.arange(row_count) // TOK_BLOCK
    dest_expert = (np.arange(wide_count)[:, None] * slots_here) // SPLIT + np.arange(experts_here)
    slot_of_row = np.broadcast_to(
        dest_expert[:, :, None, None] * CAPD + np.arange(CAPD),
        (wide_count, experts_here, blocks, CAPD),
    ).reshape(-1)
    block_of_row = np.broadcast_to(
        np.arange(blocks)[:, None], (wide_count, experts_here, blocks, CAPD)
    ).reshape(-1)
    row_slot = jnp.asarray(slot_of_row, jnp.int32)[:, None]
    same_block = jnp.asarray(block_of_row, jnp.int32)[:, None] == jnp.asarray(
        token_block, jnp.int32
    )
    first_pick = (row_slot == target[:, 0][None, :]) & same_block
    second_pick = (row_slot == target[:, 1][None, :]) & same_block
    picks = (first_pick | second_pick).astype(bf16)
    rows_per_dest = experts_here * blocks * CAPD

    full = gather_blocks(hidden, "wide").transpose(1, 0, 2).reshape(row_count, feature_count)
    normed = layer_normed(full.astype(f32), attn_gain).astype(bf16)
    normed_part = lax.dynamic_slice_in_dim(normed, wide_index * feature_share, feature_share, 1)
    kv_width = kv_here * head_size
    group_of = np.arange(wide_count) * heads_here // share
    key_term = jnp.dot(normed_part, key_weight, preferred_element_type=f32).astype(bf16)
    value_term = jnp.dot(normed_part, value_weight, preferred_element_type=f32).astype(bf16)
    kv_sent = jnp.stack(
        [
            jnp.stack(
                [
                    key_term[:, g * head_size : g * head_size + kv_width],
                    value_term[:, g * head_size : g * head_size + kv_width],
                ]
            )
            for g in group_of
        ]
    )
    kv_got = lax.all_to_all(kv_sent, "wide", split_axis=0, concat_axis=0, tiled=True)
    fresh = jnp.sum(kv_got.astype(f32), axis=0).astype(bf16)
    queries = jnp.dot(normed, query_weight, preferred_element_type=f32).astype(bf16)
    span = lax.all_gather(fresh, "narrow", axis=1, tiled=True)
    span = span.reshape(2, -1, kv_here, head_size).transpose(0, 2, 1, 3)
    own_cache_key = lax.dynamic_slice_in_dim(cache_key, kv_start, kv_here, 0)
    own_cache_value = lax.dynamic_slice_in_dim(cache_value, kv_start, kv_here, 0)
    all_keys = jnp.concatenate([own_cache_key, span[0]], axis=1)
    all_values = jnp.concatenate([own_cache_value, span[1]], axis=1)
    attended = attend(
        queries.reshape(row_count, heads_here, head_size),
        all_keys,
        all_values,
        narrow_index * row_count,
        context,
    ).reshape(row_count, heads_here * head_size)
    mix = jnp.dot(attended, out_weight, preferred_element_type=f32).astype(bf16)
    mix_sent = mix.reshape(row_count, wide_count, feature_share).transpose(1, 0, 2)
    mix_got = lax.all_to_all(mix_sent, "wide", split_axis=0, concat_axis=0, tiled=True)
    residual = (hidden.astype(f32) + jnp.sum(mix_got.astype(f32), axis=0)).astype(bf16)

    sent = jnp.dot(picks, residual, preferred_element_type=f32).astype(bf16)
    got = lax.all_to_all(
        sent.reshape(wide_count, rows_per_dest, feature_share),
        "wide",
        split_axis=0,
        concat_axis=0,
        tiled=True,
    )
    rows = got.transpose(1, 0, 2).reshape(rows_per_dest, feature_count)
    normed_two = layer_normed(rows.astype(f32), mlp_gain).astype(bf16)
    logits = jnp.dot(normed_two, router_weight, preferred_element_type=f32)
    mine = lambda values: lax.dynamic_slice_in_dim(
        values, wide_index * rows_per_dest, rows_per_dest, 0
    )
    my_first, my_second = mine(first_pick).astype(f32), mine(second_pick).astype(f32)
    ids_onehot = (expert_ids[:, :, None] == jnp.arange(experts, dtype=jnp.int32)).astype(f32)
    my_any = my_first + my_second
    first_expert = jnp.dot(my_any, ids_onehot[:, 0])
    second_expert = jnp.dot(my_any, ids_onehot[:, 1])
    leading = jax.nn.sigmoid(jnp.sum(logits * (first_expert - second_expert), axis=1))
    row_weight = jnp.where(jnp.sum(my_first, axis=1) > 0, leading, 1.0 - leading)

    tokens = gather_over_narrow(normed_two)
    tokens = tokens.reshape(narrow_count, experts_here, blocks * CAPD, feature_count)
    tokens = tokens.transpose(1, 0, 2, 3).reshape(experts_here, -1, feature_count)
    partials = []
    for e in range(experts_here):
        total = 0.0
        for p in range(parts_here):
            s = e * parts_here + p
            gate_term = jnp.dot(tokens[e], gate_weight[s], preferred_element_type=f32)
            up_term = jnp.dot(tokens[e], up_weight[s], preferred_element_type=f32)
            active = (jax.nn.silu(gate_term) * up_term).astype(bf16)
            total = total + jnp.dot(active, down_weight[s], preferred_element_type=f32)
        partials.append(total.reshape(narrow_count, blocks * CAPD, feature_count))
    partial = jnp.stack(partials, axis=1).reshape(narrow_count, rows_per_dest, feature_count)
    reduced = sum_over_narrow(partial)

    weighted = (reduced * row_weight[:, None]).astype(bf16)
    back = lax.all_to_all(
        weighted.reshape(rows_per_dest, wide_count, feature_share).transpose(1, 0, 2),
        "wide",
        split_axis=0,
        concat_axis=0,
        tiled=True,
    ).reshape(wide_count * rows_per_dest, feature_share)
    mixture = lax.dot_general(
        picks, back, (((0,), (0,)), ((), ())), preferred_element_type=f32
    )
    return (residual.astype(f32) + mixture).astype(bf16)


def solution(mesh):
    placed = (
        P("narrow", "wide"),
        P(),
        P(None, "wide"),
        P("wide", None),
        P("wide", None),
        P("wide", None),
        P(),
        P(),
        P(),
        P(),
        P("narrow", None),
        P("wide", None, "narrow"),
        P("wide", None, "narrow"),
        P("wide", "narrow", None),
    )
    return jax.shard_map(
        body, mesh=mesh, in_specs=placed, out_specs=P("narrow", "wide"), check_vma=False
    )
```

```python
import jax
import jax.numpy as jnp
import numpy as np
from jax import lax
from jax.experimental import pallas as pl
from jax.experimental.pallas import tpu as pltpu
from jax.sharding import PartitionSpec as P


SPLIT = 2
CAPD = 4
TOK_BLOCK = 16
DIRECT_LIMIT = 8
UNIT_BLOCK = 400
MIX_CHUNKS = 2
SMALL_VMEM = 24 << 20


epsilon = 1e-05


def swap(values, axis, distance):
    count = lax.axis_size(axis)
    return lax.ppermute(values, axis, [(i, i ^ distance) for i in range(count)])


def is_power_of_two(count):
    return count & (count - 1) == 0


def owners_by_distance(axis):
    count = lax.axis_size(axis)
    owners = jnp.arange(count, dtype=jnp.int32)
    return lax.axis_index(axis) ^ owners if travels_directly(axis) else owners


def travels_directly(axis):
    count = lax.axis_size(axis)
    return 2 <= count <= DIRECT_LIMIT and is_power_of_two(count)


def gather_blocks(values, axis):
    count = lax.axis_size(axis)
    if not travels_directly(axis):
        gathered = lax.all_gather(values, axis, axis=0)
        return [gathered[i] for i in range(count)]
    held = {0: values}
    for distance in range(2, count, 2):
        held[distance] = swap(values, axis, distance)
    for distance in range(1, count, 2):
        held[distance] = swap(held[distance - 1], axis, 1)
    return [held[distance] for distance in range(count)]


def sum_blocks(far, near, axis):
    f32, bf16 = jnp.float32, jnp.bfloat16
    count = lax.axis_size(axis)
    if not travels_directly(axis):
        terms = lax.all_to_all(
            jnp.concatenate([far, near]), axis, split_axis=0, concat_axis=0, tiled=True
        )
        return jnp.sum(terms.astype(f32), axis=0)
    arrived = swap(far, axis, 1)
    total = near[0].astype(f32) + arrived[0].astype(f32)
    for i in range(1, count // 2):
        term = (near[i].astype(f32) + arrived[i].astype(f32)).astype(bf16)
        total = total + swap(term, axis, 2 * i).astype(f32)
    return total


def split_order(axis):
    count = lax.axis_size(axis)
    positions = list(range(count))
    if travels_directly(axis):
        return positions[1::2], positions[0::2]
    return positions[: count // 2], positions[count // 2 :]


SMEM_SPEC = pl.BlockSpec(memory_space=pltpu.SMEM)
VMEM_SPEC = pl.BlockSpec(memory_space=pltpu.VMEM)


def row_statistics(blocks, features):
    rows = blocks[0].shape[0]
    total = jnp.zeros((rows, 1), jnp.float32)
    for block in blocks:
        total += jnp.sum(block[...].astype(jnp.float32), axis=1, keepdims=True)
    average = total / features
    square = jnp.zeros((rows, 1), jnp.float32)
    for block in blocks:
        centered = block[...].astype(jnp.float32) - average
        square += jnp.sum(centered * centered, axis=1, keepdims=True)
    return average, lax.rsqrt(square / features + epsilon)


def key_value_terms(blocks, own, gain, key_weight, value_weight, order, group_of, head_size, kv_width):
    f32, bf16 = jnp.float32, jnp.bfloat16
    rows, share = own.shape
    count = len(blocks)
    far, near = split_order("wide")
    columns = key_weight.shape[1] // head_size
    heads = kv_width // head_size

    def kernel(*refs):
        order_ref, group_ref, own_ref, gain_ref, k_ref, v_ref = refs[:6]
        block_refs = refs[6 : 6 + count]
        far_ref, near_ref, mean_ref, scale_ref, terms = refs[6 + count :]
        average, scale = row_statistics(block_refs, share * count)
        mean_ref[...] = average
        scale_ref[...] = scale
        n = ((own_ref[...].astype(f32) - average) * scale * gain_ref[...]).astype(bf16)
        for which, ref in enumerate((k_ref, v_ref)):
            term = jnp.dot(n, ref[...], preferred_element_type=f32).astype(bf16)
            for c in range(columns):
                terms[which, c] = term[:, c * head_size : (c + 1) * head_size]
        for out_ref, positions in ((far_ref, far), (near_ref, near)):
            for i, position in enumerate(positions):
                first = group_ref[order_ref[position]]
                for which in range(2):
                    for h in range(heads):
                        out_ref[i, which, :, h * head_size : (h + 1) * head_size] = terms[
                            which, first + h
                        ]

    half = jax.ShapeDtypeStruct((count // 2, 2, rows, kv_width), bf16)
    column = jax.ShapeDtypeStruct((rows, 1), f32)
    return pl.pallas_call(
        kernel,
        in_specs=[SMEM_SPEC] * 2 + [VMEM_SPEC] * (4 + count),
        out_specs=[VMEM_SPEC] * 4,
        out_shape=[half, half, column, column],
        scratch_shapes=[pltpu.VMEM((2, columns, rows, head_size), bf16)],
        compiler_params=pltpu.CompilerParams(vmem_limit_bytes=SMALL_VMEM),
        name="kv_terms",
    )(order, group_of, own, gain, key_weight, value_weight, *blocks)


def query_rows(blocks, average, scale, gain, query_weight, order):
    f32, bf16 = jnp.float32, jnp.bfloat16
    rows, share = blocks[0].shape
    count = len(blocks)
    width = query_weight.shape[1]

    def kernel(*refs):
        order_ref, mean_ref, scale_ref, gain_ref, w_ref = refs[:5]
        block_refs = refs[5 : 5 + count]
        out_ref, acc = refs[5 + count :]
        for k in range(count):
            owner = order_ref[k]
            n = (block_refs[k][...].astype(f32) - mean_ref[...]) * scale_ref[...] * gain_ref[owner]
            at = pl.multiple_of(owner * share, share)
            term = jnp.dot(n.astype(bf16), w_ref[pl.ds(at, share), :], preferred_element_type=f32)
            if k == 0:
                acc[...] = term
            else:
                acc[...] += term
        out_ref[...] = acc[...].astype(bf16)

    return pl.pallas_call(
        kernel,
        in_specs=[SMEM_SPEC] + [VMEM_SPEC] * (4 + count),
        out_specs=VMEM_SPEC,
        out_shape=jax.ShapeDtypeStruct((rows, width), bf16),
        scratch_shapes=[pltpu.VMEM((rows, width), f32)],
        compiler_params=pltpu.CompilerParams(vmem_limit_bytes=SMALL_VMEM),
        name="queries",
    )(order, average, scale, gain.reshape(count, 1, share), query_weight, *blocks)


def mix_terms(attended, out_weight, order, chunks):
    f32, bf16 = jnp.float32, jnp.bfloat16
    rows = attended.shape[0]
    count = order.shape[0]
    share = out_weight.shape[1] // count
    far, near = split_order("wide")
    half, chunk = count // 2, rows // chunks

    def kernel(order_ref, a_ref, w_ref, *out_refs):
        a = a_ref[...]
        for side, positions in enumerate((far, near)):
            for i, position in enumerate(positions):
                at = pl.multiple_of(order_ref[position] * share, share)
                term = jnp.dot(a, w_ref[:, pl.ds(at, share)], preferred_element_type=f32)
                for c in range(chunks):
                    out_refs[side * chunks + c][i] = term[c * chunk : (c + 1) * chunk].astype(bf16)

    outs = pl.pallas_call(
        kernel,
        in_specs=[SMEM_SPEC] + [VMEM_SPEC] * 2,
        out_specs=[VMEM_SPEC] * (2 * chunks),
        out_shape=[jax.ShapeDtypeStruct((half, chunk, share), bf16)] * (2 * chunks),
        compiler_params=pltpu.CompilerParams(vmem_limit_bytes=SMALL_VMEM),
        name="mix_terms",
    )(order, attended, out_weight)
    return outs[:chunks], outs[chunks:]


def normed_rows(got, gain):
    owners, rows, share = got.shape
    features = owners * share

    def kernel(x_ref, g_ref, out_ref):
        total = jnp.zeros((rows, 1), jnp.float32)
        for o in range(owners):
            total += jnp.sum(x_ref[o].astype(jnp.float32), axis=1, keepdims=True)
        average = total / features
        square = jnp.zeros((rows, 1), jnp.float32)
        for o in range(owners):
            centered = x_ref[o].astype(jnp.float32) - average
            square += jnp.sum(centered * centered, axis=1, keepdims=True)
        scale = lax.rsqrt(square / features + epsilon)
        for o in range(owners):
            at = slice(o * share, (o + 1) * share)
            centered = x_ref[o].astype(jnp.float32) - average
            out_ref[:, at] = (centered * scale * g_ref[:, at]).astype(jnp.bfloat16)

    return pl.pallas_call(
        kernel,
        out_shape=jax.ShapeDtypeStruct((rows, features), jnp.bfloat16),
        compiler_params=pltpu.CompilerParams(vmem_limit_bytes=SMALL_VMEM),
        name="normed_rows",
    )(got, gain.reshape(1, -1))


def expert_partial(pieces, gate_weight, up_weight, down_weight, first, parts):
    f32, bf16 = jnp.float32, jnp.bfloat16
    rows = sum(piece.shape[0] for piece in pieces)
    units, features = gate_weight.shape[1:]
    half = rows // 2
    block = max(b for b in range(16, units + 1, 16) if units % b == 0 and b <= UNIT_BLOCK)
    steps = units // block
    by_rows = (((1,), (1,)), ((), ()))

    def kernel(*refs):
        piece_refs = refs[: len(pieces)]
        g_ref, u_ref, d_ref, keep, send, x, acc = refs[len(pieces) :]
        p, s = pl.program_id(0), pl.program_id(1)
        starts = (p == 0) & (s == 0)

        @pl.when(starts)
        def _():
            at = 0
            for ref in piece_refs:
                x[at : at + ref.shape[0], :] = ref[...]
                at += ref.shape[0]

        tokens = x[...]
        gate = lax.dot_general(tokens, g_ref[0], by_rows, preferred_element_type=f32)
        up = lax.dot_general(tokens, u_ref[0], by_rows, preferred_element_type=f32)
        act = (jax.nn.silu(gate) * up).astype(bf16)
        out = jnp.dot(act, d_ref[0], preferred_element_type=f32)

        @pl.when(starts)
        def _():
            acc[...] = out

        @pl.when(jnp.logical_not(starts))
        def _():
            acc[...] += out

        @pl.when((p == parts - 1) & (s == steps - 1))
        def _():
            keep[...] = acc[:half].astype(bf16)
            send[...] = acc[half:].astype(bf16)

    weight_spec = pl.BlockSpec((1, block, features), lambda p, s: (first + p, s, 0))
    out_spec = pl.BlockSpec((half, features), lambda p, s: (0, 0))
    return pl.pallas_call(
        kernel,
        grid=(parts, steps),
        in_specs=[pl.BlockSpec(piece.shape, lambda p, s: (0, 0)) for piece in pieces]
        + [weight_spec] * 3,
        out_specs=[out_spec, out_spec],
        out_shape=[jax.ShapeDtypeStruct((half, features), bf16)] * 2,
        scratch_shapes=[pltpu.VMEM((rows, features), bf16), pltpu.VMEM((rows, features), f32)],
        compiler_params=pltpu.CompilerParams(
            dimension_semantics=("arbitrary", "arbitrary"), vmem_limit_bytes=48 << 20
        ),
        cost_estimate=pl.CostEstimate(
            flops=rows * features * units * 6 * parts,
            bytes_accessed=parts * 3 * features * units * 2,
            transcendentals=rows * units * parts,
        ),
        name="experts",
    )(*pieces, gate_weight, up_weight, down_weight)


def slot_targets(routing, experts, capacity):
    blocks = routing.shape[0]
    flat_ids = routing.reshape(blocks, -1)
    onehot = (flat_ids[:, :, None] == jnp.arange(experts, dtype=jnp.int32)[None, None, :]).astype(
        jnp.int32
    )
    earlier = jnp.cumsum(onehot, axis=1) - onehot
    position = jnp.sum(earlier * onehot, axis=2)
    return (flat_ids * capacity + position).reshape(routing.shape)


def attend(queries, all_keys, all_values, first_row, context):
    row_count, heads_here, head_size = queries.shape
    kv_here = all_keys.shape[0]
    grouped = queries.reshape(row_count, kv_here, heads_here // kv_here, head_size)
    scale_factor = head_size ** (-0.5)
    scores = (
        jnp.einsum("rgqd,gkd->gqrk", grouped, all_keys, preferred_element_type=jnp.float32)
        * scale_factor
    )
    row_ids = first_row + jnp.arange(row_count, dtype=jnp.int32)
    key_ids = jnp.arange(all_keys.shape[1], dtype=jnp.int32) - context
    allowed = key_ids[None, :] <= row_ids[:, None]
    scores = jnp.where(allowed[None, None], scores, -1e30)
    highest = jnp.max(scores, axis=3, keepdims=True)
    weights = jnp.exp(scores - highest)
    weights = (weights / jnp.sum(weights, axis=3, keepdims=True)).astype(jnp.bfloat16)
    mixed = jnp.einsum(
        "gqrk,gkd->rgqd", weights, all_values, preferred_element_type=jnp.float32
    ).astype(jnp.bfloat16)
    return mixed.reshape(row_count, heads_here, head_size)


def gather_pieces(rows):
    count = lax.axis_size("narrow")
    if not is_power_of_two(count) or count < 2:
        raise ValueError("narrow")
    held = {0: rows}
    distance = count // 2
    while distance >= 1:
        for have in sorted(held):
            held[have + distance] = swap(held[have], "narrow", distance)
        distance //= 2
    order = sorted(held, key=lambda d: (d & 1, d))
    return [held[d] for d in order]


def after(values, *others):
    return lax.optimization_barrier((values,) + others)[0]


def start_narrow_sum(keep, send):
    return keep.astype(jnp.float32) + swap(send, "narrow", 1).astype(jnp.float32)


def split_rows(total):
    half = total.shape[0] // 2
    return total[:half], total[half:].astype(jnp.bfloat16)


def body(
    hidden,
    attn_gain,
    query_weight,
    key_weight,
    value_weight,
    out_weight,
    cache_key,
    cache_value,
    mlp_gain,
    router_weight,
    expert_ids,
    gate_weight,
    up_weight,
    down_weight,
):
    f32, bf16 = jnp.float32, jnp.bfloat16
    wide_count = lax.axis_size("wide")
    wide_index = lax.axis_index("wide")
    narrow_index = lax.axis_index("narrow")
    narrow_count = lax.axis_size("narrow")
    row_count, feature_share = hidden.shape
    kv_total, context, head_size = cache_key.shape
    heads_here = query_weight.shape[1] // head_size
    share = heads_here * wide_count // kv_total
    kv_here = max(heads_here // share, 1)
    kv_start = wide_index * heads_here // share

    experts = router_weight.shape[1]
    slots_here = gate_weight.shape[0]
    experts_here = max(slots_here // SPLIT, 1)
    parts_here = slots_here // experts_here
    blocks = row_count // TOK_BLOCK
    routing = expert_ids.reshape(blocks, TOK_BLOCK, 2)
    target = slot_targets(routing, experts, CAPD).reshape(row_count, 2)
    token_block = np.arange(row_count) // TOK_BLOCK
    dest_expert = (np.arange(wide_count)[:, None] * slots_here) // SPLIT + np.arange(experts_here)
    slot_of_row = np.broadcast_to(
        dest_expert[:, :, None, None] * CAPD + np.arange(CAPD),
        (wide_count, experts_here, blocks, CAPD),
    ).reshape(-1)
    block_of_row = np.broadcast_to(
        np.arange(blocks)[:, None], (wide_count, experts_here, blocks, CAPD)
    ).reshape(-1)
    row_slot = jnp.asarray(slot_of_row, jnp.int32)[:, None]
    same_block = jnp.asarray(block_of_row, jnp.int32)[:, None] == jnp.asarray(
        token_block, jnp.int32
    )
    first_pick = (row_slot == target[:, 0][None, :]) & same_block
    second_pick = (row_slot == target[:, 1][None, :]) & same_block
    picks = (first_pick | second_pick).astype(bf16)

    order = owners_by_distance("wide")
    gathered = gather_blocks(hidden, "wide")
    own_gain = lax.dynamic_slice_in_dim(attn_gain, wide_index * feature_share, feature_share, 0)
    kv_width = kv_here * head_size
    group_of = jnp.arange(wide_count, dtype=jnp.int32) * heads_here // share
    far_kv, near_kv, average, scale = key_value_terms(
        gathered,
        hidden,
        own_gain.reshape(1, -1),
        key_weight,
        value_weight,
        order,
        group_of,
        head_size,
        kv_width,
    )
    fresh = sum_blocks(far_kv, near_kv, "wide").astype(bf16)
    queries = query_rows(gathered, average, scale, attn_gain, query_weight, order)
    span = lax.all_gather(fresh, "narrow", axis=1, tiled=True)
    span = span.reshape(2, -1, kv_here, head_size).transpose(0, 2, 1, 3)
    own_cache_key = lax.dynamic_slice_in_dim(cache_key, kv_start, kv_here, 0)
    own_cache_value = lax.dynamic_slice_in_dim(cache_value, kv_start, kv_here, 0)
    all_keys = jnp.concatenate([own_cache_key, span[0]], axis=1)
    all_values = jnp.concatenate([own_cache_value, span[1]], axis=1)
    attended = attend(
        queries.reshape(row_count, heads_here, head_size),
        all_keys,
        all_values,
        narrow_index * row_count,
        context,
    ).reshape(row_count, heads_here * head_size)
    far_mix, near_mix = mix_terms(attended, out_weight, order, MIX_CHUNKS)
    mixed = [sum_blocks(far, near, "wide") for far, near in zip(far_mix, near_mix)]
    residual = (hidden.astype(f32) + jnp.concatenate(mixed)).astype(bf16)

    expert_rows = blocks * CAPD
    picks = picks.reshape(wide_count, experts_here, expert_rows, row_count)
    first_pick = first_pick.astype(f32).reshape(wide_count, experts_here, expert_rows, row_count)
    second_pick = second_pick.astype(f32).reshape(wide_count, experts_here, expert_rows, row_count)
    mine = lambda values: lax.dynamic_index_in_dim(values, wide_index, 0, keepdims=False)
    my_first, my_second = mine(first_pick), mine(second_pick)
    ids_onehot = (expert_ids[:, :, None] == jnp.arange(experts, dtype=jnp.int32)).astype(f32)
    ids_diff = ids_onehot[:, 0] - ids_onehot[:, 1]

    def choose(e):
        return jnp.dot(
            picks[:, e].reshape(wide_count * expert_rows, row_count),
            residual,
            preferred_element_type=f32,
        ).astype(bf16)

    def exchange(blocks_of):
        return lax.all_to_all(blocks_of, "wide", split_axis=0, concat_axis=0, tiled=True)

    def weights_of(e, normed_two):
        logits = jnp.dot(normed_two, router_weight, preferred_element_type=f32)
        ids = jnp.dot(my_first[e] + my_second[e], ids_diff)
        leading = jax.nn.sigmoid(jnp.sum(logits * ids, axis=1))
        return jnp.where(jnp.sum(my_first[e], axis=1) > 0, leading, 1.0 - leading)

    def finish(e, own, other, distance):
        while True:
            own = own + swap(other, "narrow", distance).astype(f32)
            distance //= 2
            if distance < 2:
                break
            own, other = split_rows(own)
        weighted = (own * row_weights[e][:, None]).astype(bf16)
        back = exchange(
            weighted.reshape(expert_rows, wide_count, feature_share).transpose(1, 0, 2)
        )
        return lax.dot_general(
            picks[:, e].reshape(wide_count * expert_rows, row_count),
            back.reshape(-1, feature_share),
            (((0,), (0,)), ((), ())),
            preferred_element_type=f32,
        )

    gate_rows, up_rows = jnp.swapaxes(gate_weight, 1, 2), jnp.swapaxes(up_weight, 1, 2)
    arrived = []
    for e in range(experts_here):
        chosen = choose(e).reshape(wide_count, expert_rows, feature_share)
        arrived.append(exchange(after(chosen, *arrived[-1:])))
    normed_two = [normed_rows(got, mlp_gain) for got in arrived]
    row_weights = [weights_of(e, normed_two[e]) for e in range(experts_here)]
    pieces = [gather_pieces(rows) for rows in normed_two]
    result = residual.astype(f32)
    waiting = normed_two[1:2]
    sums = []
    for e in range(experts_here):
        tokens = [after(pieces[e][0], *waiting)] + pieces[e][1:]
        keep, far_rows = expert_partial(
            tokens, gate_rows, up_rows, down_weight, e * parts_here, parts_here
        )
        own, other = split_rows(start_narrow_sum(keep, far_rows))
        waiting = [other]
        sums.append((own, other))
    for e in range(experts_here):
        result = result + finish(e, *sums[e], narrow_count // 2)
    return result.astype(bf16)


def solution(mesh):
    placed = (
        P("narrow", "wide"),
        P(),
        P(None, "wide"),
        P("wide", None),
        P("wide", None),
        P("wide", None),
        P(),
        P(),
        P(),
        P(),
        P("narrow", None),
        P("wide", None, "narrow"),
        P("wide", None, "narrow"),
        P("wide", "narrow", None),
    )


    return jax.shard_map(
        body, mesh=mesh, in_specs=placed, out_specs=P("narrow", "wide"), check_vma=False
    )
```

```python
import jax
import jax.numpy as jnp
from jax import lax
from jax.experimental import pallas as pl
from jax.experimental.pallas import tpu as pltpu
from jax.sharding import PartitionSpec as P


SPLIT = 2
CAPD = 4
TOK_BLOCK = 16
DIRECT_LIMIT = 8
UNIT_BLOCK = 400
MIX_CHUNKS = 2
SMALL_VMEM = 24 << 20


epsilon = 1e-05


def swap(values, axis, distance):
    count = lax.axis_size(axis)
    return lax.ppermute(values, axis, [(i, i ^ distance) for i in range(count)])


def is_power_of_two(count):
    return count & (count - 1) == 0


def owners_by_distance(axis):
    count = lax.axis_size(axis)
    owners = jnp.arange(count, dtype=jnp.int32)
    return lax.axis_index(axis) ^ owners if travels_directly(axis) else owners


def travels_directly(axis):
    count = lax.axis_size(axis)
    return 2 <= count <= DIRECT_LIMIT and is_power_of_two(count)


def gather_blocks(values, axis):
    count = lax.axis_size(axis)
    if not travels_directly(axis):
        gathered = lax.all_gather(values, axis, axis=0)
        return [gathered[i] for i in range(count)]
    held = {0: values}
    for distance in sorted(range(1, count), key=lambda d: (bin(d).count("1"), -d)):
        last = distance & -distance
        held[distance] = swap(held[distance - last], axis, last)
    return [held[distance] for distance in range(count)]


def sum_blocks(far, near, axis):
    f32, bf16 = jnp.float32, jnp.bfloat16
    count = lax.axis_size(axis)
    if not travels_directly(axis):
        terms = lax.all_to_all(
            jnp.concatenate([far, near]), axis, split_axis=0, concat_axis=0, tiled=True
        )
        return jnp.sum(terms.astype(f32), axis=0)
    arrived = swap(far, axis, 1)
    total = near[0].astype(f32) + arrived[0].astype(f32)
    for i in range(1, count // 2):
        term = (near[i].astype(f32) + arrived[i].astype(f32)).astype(bf16)
        total = total + swap(term, axis, 2 * i).astype(f32)
    return total


def split_order(axis):
    count = lax.axis_size(axis)
    positions = list(range(count))
    if travels_directly(axis):
        return positions[1::2], positions[0::2]
    return positions[: count // 2], positions[count // 2 :]


SMEM_SPEC = pl.BlockSpec(memory_space=pltpu.SMEM)
VMEM_SPEC = pl.BlockSpec(memory_space=pltpu.VMEM)


def load(*arrays):
    def kernel(*refs):
        count = len(arrays)
        copies = [
            pltpu.make_async_copy(refs[i], refs[count + i], refs[2 * count].at[i])
            for i in range(count)
        ]
        for copy in copies:
            copy.start()
        for copy in copies:
            copy.wait()

    return pl.pallas_call(
        kernel,
        in_specs=[pl.BlockSpec(memory_space=pltpu.HBM)] * len(arrays),
        out_specs=[VMEM_SPEC] * len(arrays),
        out_shape=[jax.ShapeDtypeStruct(a.shape, a.dtype) for a in arrays],
        scratch_shapes=[pltpu.SemaphoreType.DMA((len(arrays),))],
        compiler_params=pltpu.CompilerParams(vmem_limit_bytes=SMALL_VMEM),
    )(*arrays)


def row_statistics(blocks, features):
    rows = blocks[0].shape[0]
    total = jnp.zeros((rows, 1), jnp.float32)
    for block in blocks:
        total += jnp.sum(block[...].astype(jnp.float32), axis=1, keepdims=True)
    average = total / features
    square = jnp.zeros((rows, 1), jnp.float32)
    for block in blocks:
        centered = block[...].astype(jnp.float32) - average
        square += jnp.sum(centered * centered, axis=1, keepdims=True)
    return average, lax.rsqrt(square / features + epsilon)


def key_value_terms(blocks, own, gain, key_weight, value_weight, order, group_of, head_size, kv_width):
    f32, bf16 = jnp.float32, jnp.bfloat16
    rows, share = own.shape
    count = len(blocks)
    far, near = split_order("wide")
    columns = key_weight.shape[1] // head_size
    heads = kv_width // head_size

    def kernel(*refs):
        order_ref, group_ref, own_ref, gain_ref, k_ref, v_ref = refs[:6]
        block_refs = refs[6 : 6 + count]
        far_ref, near_ref, mean_ref, scale_ref, terms = refs[6 + count :]
        average, scale = row_statistics(block_refs, share * count)
        mean_ref[...] = average
        scale_ref[...] = scale
        n = ((own_ref[...].astype(f32) - average) * scale * gain_ref[group_ref[count]]).astype(bf16)
        for which, ref in enumerate((k_ref, v_ref)):
            term = jnp.dot(n, ref[...], preferred_element_type=f32).astype(bf16)
            for c in range(columns):
                terms[which, c] = term[:, c * head_size : (c + 1) * head_size]
        for out_ref, positions in ((far_ref, far), (near_ref, near)):
            for i, position in enumerate(positions):
                first = group_ref[order_ref[position]]
                for which in range(2):
                    for h in range(heads):
                        out_ref[i, which, :, h * head_size : (h + 1) * head_size] = terms[
                            which, first + h
                        ]

    half = jax.ShapeDtypeStruct((count // 2, 2, rows, kv_width), bf16)
    column = jax.ShapeDtypeStruct((rows, 1), f32)
    return pl.pallas_call(
        kernel,
        in_specs=[SMEM_SPEC] * 2 + [VMEM_SPEC] * (4 + count),
        out_specs=[VMEM_SPEC] * 4,
        out_shape=[half, half, column, column],
        scratch_shapes=[pltpu.VMEM((2, columns, rows, head_size), bf16)],
        compiler_params=pltpu.CompilerParams(vmem_limit_bytes=SMALL_VMEM),
        name="kv_terms",
    )(order, group_of, own, gain, key_weight, value_weight, *blocks)


def query_rows(blocks, average, scale, gain, query_weight, order):
    f32, bf16 = jnp.float32, jnp.bfloat16
    rows, share = blocks[0].shape
    count = len(blocks)
    width = query_weight.shape[1]

    def kernel(*refs):
        order_ref, mean_ref, scale_ref, gain_ref, w_ref = refs[:5]
        block_refs = refs[5 : 5 + count]
        out_ref, acc = refs[5 + count :]
        for k in range(count):
            owner = order_ref[k]
            n = (block_refs[k][...].astype(f32) - mean_ref[...]) * scale_ref[...] * gain_ref[owner]
            at = pl.multiple_of(owner * share, share)
            term = jnp.dot(n.astype(bf16), w_ref[pl.ds(at, share), :], preferred_element_type=f32)
            if k == 0:
                acc[...] = term
            else:
                acc[...] += term
        out_ref[...] = acc[...].astype(bf16)

    return pl.pallas_call(
        kernel,
        in_specs=[SMEM_SPEC] + [VMEM_SPEC] * (4 + count),
        out_specs=VMEM_SPEC,
        out_shape=jax.ShapeDtypeStruct((rows, width), bf16),
        scratch_shapes=[pltpu.VMEM((rows, width), f32)],
        compiler_params=pltpu.CompilerParams(vmem_limit_bytes=SMALL_VMEM),
        name="queries",
    )(order, average, scale, gain, query_weight, *blocks)


def mix_terms(queries, pieces, cache_key, cache_value, out_weight, order, place, chunks):
    f32, bf16 = jnp.float32, jnp.bfloat16
    rows, inner = queries.shape
    _, head_size = cache_key.shape[1:]
    kv_here = pieces[0][1].shape[2] // head_size
    per_group = inner // head_size // kv_here
    count = order.shape[0]
    share = out_weight.shape[1] // count
    far, near = split_order("wide")
    half, chunk = count // 2, rows // chunks
    by_rows = (((1,), (1,)), ((), ()))
    distances = [distance for distance, _ in pieces]

    def kernel(order_ref, place_ref, q_ref, ck_ref, cv_ref, w_ref, *refs):
        piece_refs, out_refs, attended = refs[: len(pieces)], refs[len(pieces) : -1], refs[-1]
        here = place_ref[1]
        shape = (per_group * rows, rows)
        causal = lax.broadcasted_iota(jnp.int32, shape, 1) <= lax.rem(
            lax.broadcasted_iota(jnp.int32, shape, 0), rows
        )
        for g in range(kv_here):
            first = g * per_group
            columns = slice(g * head_size, (g + 1) * head_size)
            q = jnp.concatenate(
                [
                    q_ref[:, (first + h) * head_size : (first + h + 1) * head_size]
                    for h in range(per_group)
                ]
            )
            score = lambda keys: lax.dot_general(
                q, keys, by_rows, preferred_element_type=f32
            ) * (head_size ** (-0.5))
            scores = [score(ck_ref[place_ref[0] + g])]
            values = [cv_ref[place_ref[0] + g]]
            for distance, ref in zip(distances, piece_refs):
                allowed = causal if distance == 0 else (here ^ distance) < here
                scores.append(jnp.where(allowed, score(ref[0, :, columns]), -1e30))
                values.append(ref[1, :, columns])
            highest = scores[0].max(axis=1, keepdims=True)
            for s in scores[1:]:
                highest = jnp.maximum(highest, s.max(axis=1, keepdims=True))
            weights = [jnp.exp(s - highest) for s in scores]
            total = sum(w.sum(axis=1, keepdims=True) for w in weights)
            mixed = sum(
                jnp.dot((w / total).astype(bf16), v, preferred_element_type=f32)
                for w, v in zip(weights, values)
            ).astype(bf16)
            for h in range(per_group):
                attended[:, (first + h) * head_size : (first + h + 1) * head_size] = mixed[
                    h * rows : (h + 1) * rows
                ]
        a = attended[...]
        for side, positions in enumerate((far, near)):
            for i, position in enumerate(positions):
                at = pl.multiple_of(order_ref[position] * share, share)
                term = jnp.dot(a, w_ref[:, pl.ds(at, share)], preferred_element_type=f32)
                for c in range(chunks):
                    out_refs[side * chunks + c][i] = term[c * chunk : (c + 1) * chunk].astype(bf16)

    outs = pl.pallas_call(
        kernel,
        in_specs=[SMEM_SPEC] * 2 + [VMEM_SPEC] * (4 + len(pieces)),
        out_specs=[VMEM_SPEC] * (2 * chunks),
        out_shape=[jax.ShapeDtypeStruct((half, chunk, share), bf16)] * (2 * chunks),
        scratch_shapes=[pltpu.VMEM((rows, inner), bf16)],
        compiler_params=pltpu.CompilerParams(vmem_limit_bytes=SMALL_VMEM),
        name="mix_terms",
    )(order, place, queries, cache_key, cache_value, out_weight, *[p for _, p in pieces])
    return outs[:chunks], outs[chunks:]


def normed_rows(got, gain):
    owners, rows, share = got.shape
    features = owners * share

    def kernel(x_ref, g_ref, out_ref):
        blocks = [x_ref.at[o] for o in range(owners)]
        average, scale = row_statistics(blocks, features)
        for o, block in enumerate(blocks):
            at = slice(o * share, (o + 1) * share)
            centered = block[...].astype(jnp.float32) - average
            out_ref[:, at] = (centered * scale * g_ref[:, at]).astype(jnp.bfloat16)

    return pl.pallas_call(
        kernel,
        in_specs=[VMEM_SPEC] * 2,
        out_specs=VMEM_SPEC,
        out_shape=jax.ShapeDtypeStruct((rows, features), jnp.bfloat16),
        compiler_params=pltpu.CompilerParams(vmem_limit_bytes=SMALL_VMEM),
        name="normed_rows",
    )(got, gain)


def cut_rows(rows, weights, count):
    share = rows[0].shape[1] // count
    total = sum(r.shape[0] for r in rows)

    def kernel(*refs):
        out_ref = refs[-1]
        at = 0
        for x_ref, w_ref in zip(refs[: len(rows)], refs[len(rows) : -1]):
            for o in range(count):
                block = x_ref[:, o * share : (o + 1) * share] * w_ref[...]
                out_ref[o, at : at + x_ref.shape[0]] = block.astype(jnp.bfloat16)
            at += x_ref.shape[0]

    return pl.pallas_call(
        kernel,
        in_specs=[VMEM_SPEC] * (2 * len(rows)),
        out_specs=VMEM_SPEC,
        out_shape=jax.ShapeDtypeStruct((count, total, share), jnp.bfloat16),
        compiler_params=pltpu.CompilerParams(vmem_limit_bytes=SMALL_VMEM),
        name="cut_rows",
    )(*rows, *weights)


def expert_partial(pieces, gate_weight, up_weight, down_weight, first, parts):
    f32, bf16 = jnp.float32, jnp.bfloat16
    rows = sum(piece.shape[0] for piece in pieces)
    units, features = gate_weight.shape[1:]
    half = rows // 2
    block = max(b for b in range(16, units + 1, 16) if units % b == 0 and b <= UNIT_BLOCK)
    steps = units // block
    by_rows = (((1,), (1,)), ((), ()))

    def kernel(*refs):
        piece_refs = refs[: len(pieces)]
        g_ref, u_ref, d_ref, keep, send, x, acc = refs[len(pieces) :]
        p, s = pl.program_id(0), pl.program_id(1)
        starts = (p == 0) & (s == 0)

        @pl.when(starts)
        def _():
            at = 0
            for ref in piece_refs:
                x[at : at + ref.shape[0], :] = ref[...]
                at += ref.shape[0]

        tokens = x[...]
        gate = lax.dot_general(tokens, g_ref[0], by_rows, preferred_element_type=f32)
        up = lax.dot_general(tokens, u_ref[0], by_rows, preferred_element_type=f32)
        act = (jax.nn.silu(gate) * up).astype(bf16)
        out = jnp.dot(act, d_ref[0], preferred_element_type=f32)

        @pl.when(starts)
        def _():
            acc[...] = out

        @pl.when(jnp.logical_not(starts))
        def _():
            acc[...] += out

        @pl.when((p == parts - 1) & (s == steps - 1))
        def _():
            keep[...] = acc[:half].astype(bf16)
            send[...] = acc[half:].astype(bf16)

    weight_spec = pl.BlockSpec((1, block, features), lambda p, s: (first + p, s, 0))
    out_spec = pl.BlockSpec((half, features), lambda p, s: (0, 0))
    return pl.pallas_call(
        kernel,
        grid=(parts, steps),
        in_specs=[pl.BlockSpec(piece.shape, lambda p, s: (0, 0)) for piece in pieces]
        + [weight_spec] * 3,
        out_specs=[out_spec, out_spec],
        out_shape=[jax.ShapeDtypeStruct((half, features), bf16)] * 2,
        scratch_shapes=[pltpu.VMEM((rows, features), bf16), pltpu.VMEM((rows, features), f32)],
        compiler_params=pltpu.CompilerParams(
            dimension_semantics=("arbitrary", "arbitrary"), vmem_limit_bytes=48 << 20
        ),
        cost_estimate=pl.CostEstimate(
            flops=rows * features * units * 6 * parts,
            bytes_accessed=parts * 3 * features * units * 2,
            transcendentals=rows * units * parts,
        ),
        name="experts",
    )(*pieces, gate_weight, up_weight, down_weight)


def slot_targets(routing, experts, capacity):
    blocks = routing.shape[0]
    flat_ids = routing.reshape(blocks, -1)
    onehot = (flat_ids[:, :, None] == jnp.arange(experts, dtype=jnp.int32)[None, None, :]).astype(
        jnp.int32
    )
    earlier = jnp.cumsum(onehot, axis=1) - onehot
    position = jnp.sum(earlier * onehot, axis=2)
    return (flat_ids * capacity + position).reshape(routing.shape)


def gather_pieces(rows):
    count = lax.axis_size("narrow")
    if not is_power_of_two(count) or count < 2:
        raise ValueError("narrow")
    held = {0: rows}
    distance = count // 2
    while distance >= 1:
        for have in sorted(held):
            held[have + distance] = swap(held[have], "narrow", distance)
        distance //= 2
    order = sorted(held, key=lambda d: (d & 1, d))
    return [held[d] for d in order]


def after(values, *others):
    return lax.optimization_barrier((values,) + others)[0]


def start_narrow_sum(keep, send):
    return keep.astype(jnp.float32) + swap(send, "narrow", 1).astype(jnp.float32)


def split_rows(total):
    half = total.shape[0] // 2
    return total[:half], total[half:].astype(jnp.bfloat16)


def body(
    hidden,
    attn_gain,
    query_weight,
    key_weight,
    value_weight,
    out_weight,
    cache_key,
    cache_value,
    mlp_gain,
    router_weight,
    expert_ids,
    gate_weight,
    up_weight,
    down_weight,
):
    f32, bf16 = jnp.float32, jnp.bfloat16
    wide_count = lax.axis_size("wide")
    wide_index = lax.axis_index("wide")
    narrow_index = lax.axis_index("narrow")
    narrow_count = lax.axis_size("narrow")
    row_count, feature_share = hidden.shape
    kv_total, _, head_size = cache_key.shape
    heads_here = query_weight.shape[1] // head_size
    share = heads_here * wide_count // kv_total
    kv_here = max(heads_here // share, 1)
    kv_start = wide_index * heads_here // share

    experts = router_weight.shape[1]
    slots_here = gate_weight.shape[0]
    experts_here = max(slots_here // SPLIT, 1)
    parts_here = slots_here // experts_here
    blocks = row_count // TOK_BLOCK
    order = owners_by_distance("wide")
    gathered = gather_blocks(hidden, "wide")
    gain_blocks = attn_gain.reshape(wide_count, 1, feature_share)
    key_weight, value_weight, gain_blocks, own_block = load(
        key_weight, value_weight, gain_blocks, hidden
    )
    if travels_directly("wide"):
        gathered[0] = own_block
    kv_width = kv_here * head_size
    group_of = jnp.arange(wide_count, dtype=jnp.int32) * heads_here // share
    far_kv, near_kv, average, scale = key_value_terms(
        gathered,
        own_block,
        gain_blocks,
        key_weight,
        value_weight,
        order,
        jnp.append(group_of, wide_index).astype(jnp.int32),
        head_size,
        kv_width,
    )
    cache_key, cache_value, mlp_gain_row = load(cache_key, cache_value, mlp_gain.reshape(1, -1))
    fresh = sum_blocks(far_kv, near_kv, "wide").astype(bf16)
    queries = query_rows(gathered, average, scale, gain_blocks, query_weight, order)
    span = gather_pieces(fresh)
    distances = sorted(range(narrow_count), key=lambda d: (d & 1, d))
    far_mix, near_mix = mix_terms(
        queries,
        list(zip(distances, span)),
        cache_key,
        cache_value,
        out_weight,
        order,
        jnp.stack([kv_start, narrow_index]).astype(jnp.int32),
        MIX_CHUNKS,
    )
    expert_ids = after(expert_ids, far_mix[0])
    routing = expert_ids.reshape(blocks, TOK_BLOCK, 2)
    target = slot_targets(routing, experts, CAPD).reshape(row_count, 2)
    token_block = jnp.arange(row_count, dtype=jnp.int32) // TOK_BLOCK
    dest_expert = (jnp.arange(wide_count, dtype=jnp.int32) * slots_here // SPLIT)[:, None] + jnp.arange(
        experts_here, dtype=jnp.int32
    )
    expert_rows = blocks * CAPD
    in_expert = jnp.arange(expert_rows, dtype=jnp.int32)
    row_slot = dest_expert[:, :, None, None] * CAPD + (in_expert % CAPD)[:, None]
    same_block = (in_expert // CAPD)[:, None] == token_block
    first_pick = (row_slot == target[:, 0]) & same_block
    second_pick = (row_slot == target[:, 1]) & same_block
    picks = lax.optimization_barrier((first_pick | second_pick).astype(bf16))
    mixed = [sum_blocks(far, near, "wide") for far, near in zip(far_mix, near_mix)]
    residual = (hidden.astype(f32) + jnp.concatenate(mixed)).astype(bf16)

    mine = lambda values: lax.dynamic_index_in_dim(
        values.astype(f32), wide_index, 0, keepdims=False
    )
    my_first, my_second = mine(first_pick), mine(second_pick)
    ids_onehot = (expert_ids[:, :, None] == jnp.arange(experts, dtype=jnp.int32)).astype(f32)
    ids_diff = ids_onehot[:, 0] - ids_onehot[:, 1]

    def exchange(blocks_of):
        return lax.all_to_all(blocks_of, "wide", split_axis=0, concat_axis=0, tiled=True)

    def weights_of(e, normed_two):
        logits = jnp.dot(normed_two, router_weight, preferred_element_type=f32)
        ids = jnp.dot(my_first[e] + my_second[e], ids_diff)
        leading = jax.nn.sigmoid(jnp.sum(logits * ids, axis=1))
        return jnp.where(jnp.sum(my_first[e], axis=1) > 0, leading, 1.0 - leading)

    def finish(own, other, distance):
        while True:
            own = own + swap(other, "narrow", distance).astype(f32)
            distance //= 2
            if distance < 2:
                break
            own, other = split_rows(own)
        return own

    gate_rows, up_rows = jnp.swapaxes(gate_weight, 1, 2), jnp.swapaxes(up_weight, 1, 2)
    chosen = jnp.dot(
        picks.transpose(1, 0, 2, 3).reshape(-1, row_count), residual, preferred_element_type=f32
    ).astype(bf16)
    chosen = chosen.reshape(experts_here, wide_count, expert_rows, feature_share)
    arrived = []
    for e in range(experts_here):
        arrived.append(exchange(after(chosen[e], *arrived[-1:])))
    normed_two = [normed_rows(got, mlp_gain_row) for got in arrived]
    row_weights = [weights_of(e, normed_two[e]) for e in range(experts_here)]
    pieces = [gather_pieces(rows) for rows in normed_two]
    waiting = []
    sums = []
    for e in range(experts_here):
        tokens = [after(pieces[e][0], *waiting)] + pieces[e][1:]
        keep, far_rows = expert_partial(
            tokens, gate_rows, up_rows, down_weight, e * parts_here, parts_here
        )
        own, other = split_rows(start_narrow_sum(keep, far_rows))
        waiting = [other]
        sums.append((own, other))
    own_rows = [finish(*sums[e], narrow_count // 2) for e in range(experts_here)]
    back = exchange(cut_rows(own_rows, [w[:, None] for w in row_weights], wide_count))
    mixture = lax.dot_general(
        picks.reshape(-1, row_count),
        back.reshape(-1, feature_share),
        (((0,), (0,)), ((), ())),
        preferred_element_type=f32,
    )
    return (residual.astype(f32) + mixture).astype(bf16)


def solution(mesh):
    placed = (
        P("narrow", "wide"),
        P(),
        P(None, "wide"),
        P("wide", None),
        P("wide", None),
        P("wide", None),
        P(),
        P(),
        P(),
        P(),
        P("narrow", None),
        P("wide", None, "narrow"),
        P("wide", None, "narrow"),
        P("wide", "narrow", None),
    )


    return jax.shard_map(
        body, mesh=mesh, in_specs=placed, out_specs=P("narrow", "wide"), check_vma=False
    )
```

```python
import jax
import jax.numpy as jnp
from jax import lax
from jax.experimental import pallas as pl
from jax.experimental.pallas import tpu as pltpu
from jax.sharding import PartitionSpec as P


SPLIT = 2
CAPD = 4
TOK_BLOCK = 16
DIRECT_LIMIT = 8
UNIT_BLOCK = 400
MIX_CHUNKS = 2
SMALL_VMEM = 24 << 20


epsilon = 1e-05


def swap(values, axis, distance):
    count = lax.axis_size(axis)
    return lax.ppermute(values, axis, [(i, i ^ distance) for i in range(count)])


def is_power_of_two(count):
    return count & (count - 1) == 0


def owners_by_distance(axis):
    count = lax.axis_size(axis)
    owners = jnp.arange(count, dtype=jnp.int32)
    return lax.axis_index(axis) ^ owners if travels_directly(axis) else owners


def travels_directly(axis):
    count = lax.axis_size(axis)
    return 2 <= count <= DIRECT_LIMIT and is_power_of_two(count)


def gather_blocks(values, axis):
    count = lax.axis_size(axis)
    if not travels_directly(axis):
        gathered = lax.all_gather(values, axis, axis=0)
        return [gathered[i] for i in range(count)]
    held = {0: values}
    for distance in sorted(range(1, count), key=lambda d: (bin(d).count("1"), -d)):
        last = distance & -distance
        held[distance] = swap(held[distance - last], axis, last)
    return [held[distance] for distance in range(count)]


def sum_blocks(far, near, axis):
    f32, bf16 = jnp.float32, jnp.bfloat16
    count = lax.axis_size(axis)
    if not travels_directly(axis):
        terms = lax.all_to_all(
            jnp.concatenate([far, near]), axis, split_axis=0, concat_axis=0, tiled=True
        )
        return jnp.sum(terms.astype(f32), axis=0)
    arrived = swap(far, axis, 1)
    total = near[0].astype(f32) + arrived[0].astype(f32)
    for i in range(1, count // 2):
        term = (near[i].astype(f32) + arrived[i].astype(f32)).astype(bf16)
        total = total + swap(term, axis, 2 * i).astype(f32)
    return total


def split_order(axis):
    count = lax.axis_size(axis)
    positions = list(range(count))
    if travels_directly(axis):
        return positions[1::2], positions[0::2]
    return positions[: count // 2], positions[count // 2 :]


SMEM_SPEC = pl.BlockSpec(memory_space=pltpu.SMEM)
VMEM_SPEC = pl.BlockSpec(memory_space=pltpu.VMEM)


def load(*arrays):
    def kernel(*refs):
        count = len(arrays)
        copies = [
            pltpu.make_async_copy(refs[i], refs[count + i], refs[2 * count].at[i])
            for i in range(count)
        ]
        for copy in copies:
            copy.start()
        for copy in copies:
            copy.wait()

    return pl.pallas_call(
        kernel,
        in_specs=[pl.BlockSpec(memory_space=pltpu.HBM)] * len(arrays),
        out_specs=[VMEM_SPEC] * len(arrays),
        out_shape=[jax.ShapeDtypeStruct(a.shape, a.dtype) for a in arrays],
        scratch_shapes=[pltpu.SemaphoreType.DMA((len(arrays),))],
        compiler_params=pltpu.CompilerParams(vmem_limit_bytes=SMALL_VMEM),
    )(*arrays)


def row_statistics(blocks, features):
    rows = blocks[0].shape[0]
    total = jnp.zeros((rows, 1), jnp.float32)
    for block in blocks:
        total += jnp.sum(block[...].astype(jnp.float32), axis=1, keepdims=True)
    average = total / features
    square = jnp.zeros((rows, 1), jnp.float32)
    for block in blocks:
        centered = block[...].astype(jnp.float32) - average
        square += jnp.sum(centered * centered, axis=1, keepdims=True)
    return average, lax.rsqrt(square / features + epsilon)


def key_value_terms(blocks, own, gain, key_weight, value_weight, order, group_of, head_size, kv_width):
    f32, bf16 = jnp.float32, jnp.bfloat16
    rows, share = own.shape
    count = len(blocks)
    far, near = split_order("wide")
    columns = key_weight.shape[1] // head_size
    heads = kv_width // head_size

    def kernel(*refs):
        order_ref, group_ref, own_ref, gain_ref, k_ref, v_ref = refs[:6]
        block_refs = refs[6 : 6 + count]
        far_ref, near_ref, mean_ref, scale_ref, terms = refs[6 + count :]
        average, scale = row_statistics(block_refs, share * count)
        mean_ref[...] = average
        scale_ref[...] = scale
        n = ((own_ref[...].astype(f32) - average) * scale * gain_ref[group_ref[count]]).astype(bf16)
        for which, ref in enumerate((k_ref, v_ref)):
            term = jnp.dot(n, ref[...], preferred_element_type=f32).astype(bf16)
            for c in range(columns):
                terms[which, c] = term[:, c * head_size : (c + 1) * head_size]
        for out_ref, positions in ((far_ref, far), (near_ref, near)):
            for i, position in enumerate(positions):
                first = group_ref[order_ref[position]]
                for which in range(2):
                    for h in range(heads):
                        out_ref[i, which, :, h * head_size : (h + 1) * head_size] = terms[
                            which, first + h
                        ]

    half = jax.ShapeDtypeStruct((count // 2, 2, rows, kv_width), bf16)
    column = jax.ShapeDtypeStruct((rows, 1), f32)
    return pl.pallas_call(
        kernel,
        in_specs=[SMEM_SPEC] * 2 + [VMEM_SPEC] * (4 + count),
        out_specs=[VMEM_SPEC] * 4,
        out_shape=[half, half, column, column],
        scratch_shapes=[pltpu.VMEM((2, columns, rows, head_size), bf16)],
        compiler_params=pltpu.CompilerParams(vmem_limit_bytes=SMALL_VMEM),
        name="kv_terms",
    )(order, group_of, own, gain, key_weight, value_weight, *blocks)


def query_rows(blocks, average, scale, gain, query_weight, order):
    f32, bf16 = jnp.float32, jnp.bfloat16
    rows, share = blocks[0].shape
    count = len(blocks)
    width = query_weight.shape[1]

    def kernel(*refs):
        order_ref, mean_ref, scale_ref, gain_ref, w_ref = refs[:5]
        block_refs = refs[5 : 5 + count]
        out_ref, acc = refs[5 + count :]
        for k in range(count):
            owner = order_ref[k]
            n = (block_refs[k][...].astype(f32) - mean_ref[...]) * scale_ref[...] * gain_ref[owner]
            at = pl.multiple_of(owner * share, share)
            term = jnp.dot(n.astype(bf16), w_ref[pl.ds(at, share), :], preferred_element_type=f32)
            if k == 0:
                acc[...] = term
            else:
                acc[...] += term
        out_ref[...] = acc[...].astype(bf16)

    return pl.pallas_call(
        kernel,
        in_specs=[SMEM_SPEC] + [VMEM_SPEC] * (4 + count),
        out_specs=VMEM_SPEC,
        out_shape=jax.ShapeDtypeStruct((rows, width), bf16),
        scratch_shapes=[pltpu.VMEM((rows, width), f32)],
        compiler_params=pltpu.CompilerParams(vmem_limit_bytes=SMALL_VMEM),
        name="queries",
    )(order, average, scale, gain, query_weight, *blocks)


def mix_terms(queries, pieces, cache_key, cache_value, out_weight, order, place, chunks):
    f32, bf16 = jnp.float32, jnp.bfloat16
    rows, inner = queries.shape
    _, head_size = cache_key.shape[1:]
    kv_here = pieces[0][1].shape[2] // head_size
    per_group = inner // head_size // kv_here
    count = order.shape[0]
    share = out_weight.shape[1] // count
    far, near = split_order("wide")
    half, chunk = count // 2, rows // chunks
    by_rows = (((1,), (1,)), ((), ()))
    distances = [distance for distance, _ in pieces]

    def kernel(order_ref, place_ref, q_ref, ck_ref, cv_ref, w_ref, *refs):
        piece_refs, out_refs, attended = refs[: len(pieces)], refs[len(pieces) : -1], refs[-1]
        here = place_ref[1]
        shape = (per_group * rows, rows)
        causal = lax.broadcasted_iota(jnp.int32, shape, 1) <= lax.rem(
            lax.broadcasted_iota(jnp.int32, shape, 0), rows
        )
        for g in range(kv_here):
            first = g * per_group
            columns = slice(g * head_size, (g + 1) * head_size)
            q = jnp.concatenate(
                [
                    q_ref[:, (first + h) * head_size : (first + h + 1) * head_size]
                    for h in range(per_group)
                ]
            )
            score = lambda keys: lax.dot_general(
                q, keys, by_rows, preferred_element_type=f32
            ) * (head_size ** (-0.5))
            scores = [score(ck_ref[place_ref[0] + g])]
            values = [cv_ref[place_ref[0] + g]]
            for distance, ref in zip(distances, piece_refs):
                allowed = causal if distance == 0 else (here ^ distance) < here
                scores.append(jnp.where(allowed, score(ref[0, :, columns]), -1e30))
                values.append(ref[1, :, columns])
            highest = scores[0].max(axis=1, keepdims=True)
            for s in scores[1:]:
                highest = jnp.maximum(highest, s.max(axis=1, keepdims=True))
            weights = [jnp.exp(s - highest) for s in scores]
            total = sum(w.sum(axis=1, keepdims=True) for w in weights)
            mixed = sum(
                jnp.dot((w / total).astype(bf16), v, preferred_element_type=f32)
                for w, v in zip(weights, values)
            ).astype(bf16)
            for h in range(per_group):
                attended[:, (first + h) * head_size : (first + h + 1) * head_size] = mixed[
                    h * rows : (h + 1) * rows
                ]
        a = attended[...]
        for side, positions in enumerate((far, near)):
            for i, position in enumerate(positions):
                at = pl.multiple_of(order_ref[position] * share, share)
                term = jnp.dot(a, w_ref[:, pl.ds(at, share)], preferred_element_type=f32)
                for c in range(chunks):
                    out_refs[side * chunks + c][i] = term[c * chunk : (c + 1) * chunk].astype(bf16)

    outs = pl.pallas_call(
        kernel,
        in_specs=[SMEM_SPEC] * 2 + [VMEM_SPEC] * (4 + len(pieces)),
        out_specs=[VMEM_SPEC] * (2 * chunks),
        out_shape=[jax.ShapeDtypeStruct((half, chunk, share), bf16)] * (2 * chunks),
        scratch_shapes=[pltpu.VMEM((rows, inner), bf16)],
        compiler_params=pltpu.CompilerParams(vmem_limit_bytes=SMALL_VMEM),
        name="mix_terms",
    )(order, place, queries, cache_key, cache_value, out_weight, *[p for _, p in pieces])
    return outs[:chunks], outs[chunks:]


def normed_rows(got, gain):
    owners, rows, share = got.shape
    features = owners * share

    def kernel(x_ref, g_ref, out_ref):
        blocks = [x_ref.at[o] for o in range(owners)]
        average, scale = row_statistics(blocks, features)
        for o, block in enumerate(blocks):
            at = slice(o * share, (o + 1) * share)
            centered = block[...].astype(jnp.float32) - average
            out_ref[:, at] = (centered * scale * g_ref[:, at]).astype(jnp.bfloat16)

    return pl.pallas_call(
        kernel,
        in_specs=[VMEM_SPEC] * 2,
        out_specs=VMEM_SPEC,
        out_shape=jax.ShapeDtypeStruct((rows, features), jnp.bfloat16),
        compiler_params=pltpu.CompilerParams(vmem_limit_bytes=SMALL_VMEM),
        name="normed_rows",
    )(got, gain)


def cut_rows(rows, weights, count):
    share = rows[0].shape[1] // count
    total = sum(r.shape[0] for r in rows)

    def kernel(*refs):
        out_ref = refs[-1]
        at = 0
        for x_ref, w_ref in zip(refs[: len(rows)], refs[len(rows) : -1]):
            for o in range(count):
                block = x_ref[:, o * share : (o + 1) * share] * w_ref[...]
                out_ref[o, at : at + x_ref.shape[0]] = block.astype(jnp.bfloat16)
            at += x_ref.shape[0]

    return pl.pallas_call(
        kernel,
        in_specs=[VMEM_SPEC] * (2 * len(rows)),
        out_specs=VMEM_SPEC,
        out_shape=jax.ShapeDtypeStruct((count, total, share), jnp.bfloat16),
        compiler_params=pltpu.CompilerParams(vmem_limit_bytes=SMALL_VMEM),
        name="cut_rows",
    )(*rows, *weights)


def expert_partial(pieces, gate_weight, up_weight, down_weight, first, parts):
    f32, bf16 = jnp.float32, jnp.bfloat16
    rows = sum(piece.shape[0] for piece in pieces)
    units, features = gate_weight.shape[1:]
    half = rows // 2
    block = max(b for b in range(16, units + 1, 16) if units % b == 0 and b <= UNIT_BLOCK)
    steps = units // block
    by_rows = (((1,), (1,)), ((), ()))

    def kernel(*refs):
        piece_refs = refs[: len(pieces)]
        g_ref, u_ref, d_ref, keep, send, x, acc = refs[len(pieces) :]
        p, s = pl.program_id(0), pl.program_id(1)
        starts = (p == 0) & (s == 0)

        @pl.when(starts)
        def _():
            at = 0
            for ref in piece_refs:
                x[at : at + ref.shape[0], :] = ref[...]
                at += ref.shape[0]

        tokens = x[...]
        gate = lax.dot_general(tokens, g_ref[0], by_rows, preferred_element_type=f32)
        up = lax.dot_general(tokens, u_ref[0], by_rows, preferred_element_type=f32)
        act = (jax.nn.silu(gate) * up).astype(bf16)
        out = jnp.dot(act, d_ref[0], preferred_element_type=f32)

        @pl.when(starts)
        def _():
            acc[...] = out

        @pl.when(jnp.logical_not(starts))
        def _():
            acc[...] += out

        @pl.when((p == parts - 1) & (s == steps - 1))
        def _():
            keep[...] = acc[:half].astype(bf16)
            send[...] = acc[half:].astype(bf16)

    weight_spec = pl.BlockSpec((1, block, features), lambda p, s: (first + p, s, 0))
    out_spec = pl.BlockSpec((half, features), lambda p, s: (0, 0))
    return pl.pallas_call(
        kernel,
        grid=(parts, steps),
        in_specs=[pl.BlockSpec(piece.shape, lambda p, s: (0, 0)) for piece in pieces]
        + [weight_spec] * 3,
        out_specs=[out_spec, out_spec],
        out_shape=[jax.ShapeDtypeStruct((half, features), bf16)] * 2,
        scratch_shapes=[pltpu.VMEM((rows, features), bf16), pltpu.VMEM((rows, features), f32)],
        compiler_params=pltpu.CompilerParams(
            dimension_semantics=("arbitrary", "arbitrary"), vmem_limit_bytes=48 << 20
        ),
        cost_estimate=pl.CostEstimate(
            flops=rows * features * units * 6 * parts,
            bytes_accessed=parts * 3 * features * units * 2,
            transcendentals=rows * units * parts,
        ),
        name="experts",
    )(*pieces, gate_weight, up_weight, down_weight)


def slot_targets(routing, experts, capacity):
    blocks = routing.shape[0]
    flat_ids = routing.reshape(blocks, -1)
    onehot = (flat_ids[:, :, None] == jnp.arange(experts, dtype=jnp.int32)[None, None, :]).astype(
        jnp.int32
    )
    earlier = jnp.cumsum(onehot, axis=1) - onehot
    position = jnp.sum(earlier * onehot, axis=2)
    return (flat_ids * capacity + position).reshape(routing.shape)


def gather_pieces(rows):
    count = lax.axis_size("narrow")
    if not is_power_of_two(count) or count < 2:
        raise ValueError("narrow")
    held = {0: rows}
    distance = count // 2
    while distance >= 1:
        for have in sorted(held):
            held[have + distance] = swap(held[have], "narrow", distance)
        distance //= 2
    order = sorted(held, key=lambda d: (d & 1, d))
    return [held[d] for d in order]


def after(values, *others):
    return lax.optimization_barrier((values,) + others)[0]


def start_narrow_sum(keep, send):
    return keep.astype(jnp.float32) + swap(send, "narrow", 1).astype(jnp.float32)


def split_rows(total):
    half = total.shape[0] // 2
    return total[:half], total[half:].astype(jnp.bfloat16)


def body(
    hidden,
    attn_gain,
    query_weight,
    key_weight,
    value_weight,
    out_weight,
    cache_key,
    cache_value,
    mlp_gain,
    router_weight,
    expert_ids,
    gate_weight,
    up_weight,
    down_weight,
):
    f32, bf16 = jnp.float32, jnp.bfloat16
    wide_count = lax.axis_size("wide")
    wide_index = lax.axis_index("wide")
    narrow_index = lax.axis_index("narrow")
    narrow_count = lax.axis_size("narrow")
    row_count, feature_share = hidden.shape
    kv_total, _, head_size = cache_key.shape
    heads_here = query_weight.shape[1] // head_size
    share = heads_here * wide_count // kv_total
    kv_here = max(heads_here // share, 1)
    kv_start = wide_index * heads_here // share

    experts = router_weight.shape[1]
    slots_here = gate_weight.shape[0]
    experts_here = max(slots_here // SPLIT, 1)
    parts_here = slots_here // experts_here
    blocks = row_count // TOK_BLOCK
    order = owners_by_distance("wide")
    gathered = gather_blocks(hidden, "wide")
    gain_blocks = attn_gain.reshape(wide_count, 1, feature_share)
    key_weight, value_weight, gain_blocks, own_block = load(
        key_weight, value_weight, gain_blocks, hidden
    )
    if travels_directly("wide"):
        gathered[0] = own_block
    kv_width = kv_here * head_size
    group_of = jnp.arange(wide_count, dtype=jnp.int32) * heads_here // share
    far_kv, near_kv, average, scale = key_value_terms(
        gathered,
        own_block,
        gain_blocks,
        key_weight,
        value_weight,
        order,
        jnp.append(group_of, wide_index).astype(jnp.int32),
        head_size,
        kv_width,
    )
    cache_key, cache_value, mlp_gain_row = load(cache_key, cache_value, mlp_gain.reshape(1, -1))
    fresh = sum_blocks(far_kv, near_kv, "wide").astype(bf16)
    queries = query_rows(gathered, average, scale, gain_blocks, query_weight, order)
    span = gather_pieces(fresh)
    distances = sorted(range(narrow_count), key=lambda d: (d & 1, d))
    far_mix, near_mix = mix_terms(
        queries,
        list(zip(distances, span)),
        cache_key,
        cache_value,
        out_weight,
        order,
        jnp.stack([kv_start, narrow_index]).astype(jnp.int32),
        MIX_CHUNKS,
    )
    expert_ids = after(expert_ids, far_mix[0])
    routing = expert_ids.reshape(blocks, TOK_BLOCK, 2)
    target = slot_targets(routing, experts, CAPD).reshape(row_count, 2)
    token_block = jnp.arange(row_count, dtype=jnp.int32) // TOK_BLOCK
    dest_expert = jnp.arange(wide_count, dtype=jnp.int32) * slots_here // SPLIT + jnp.arange(
        experts_here, dtype=jnp.int32
    )[:, None]
    expert_rows = blocks * CAPD
    in_expert = jnp.arange(expert_rows, dtype=jnp.int32)
    row_slot = dest_expert[:, :, None, None] * CAPD + (in_expert % CAPD)[:, None]
    same_block = (in_expert // CAPD)[:, None] == token_block
    first_pick = (row_slot == target[:, 0]) & same_block
    second_pick = (row_slot == target[:, 1]) & same_block
    picks = lax.optimization_barrier((first_pick | second_pick).astype(bf16))
    mixed = [sum_blocks(far, near, "wide") for far, near in zip(far_mix, near_mix)]
    residual = (hidden.astype(f32) + jnp.concatenate(mixed)).astype(bf16)

    mine = lambda values: lax.dynamic_index_in_dim(
        values.astype(f32), wide_index, 1, keepdims=False
    )
    my_first, my_second = mine(first_pick), mine(second_pick)
    ids_onehot = (expert_ids[:, :, None] == jnp.arange(experts, dtype=jnp.int32)).astype(f32)
    ids_diff = ids_onehot[:, 0] - ids_onehot[:, 1]

    def exchange(blocks_of):
        return lax.all_to_all(blocks_of, "wide", split_axis=0, concat_axis=0, tiled=True)

    def weights_of(e, normed_two):
        logits = jnp.dot(normed_two, router_weight, preferred_element_type=f32)
        ids = jnp.dot(my_first[e] + my_second[e], ids_diff)
        leading = jax.nn.sigmoid(jnp.sum(logits * ids, axis=1))
        return jnp.where(jnp.sum(my_first[e], axis=1) > 0, leading, 1.0 - leading)

    def finish(own, other, distance):
        while True:
            own = own + swap(other, "narrow", distance).astype(f32)
            distance //= 2
            if distance < 2:
                break
            own, other = split_rows(own)
        return own

    gate_rows, up_rows = jnp.swapaxes(gate_weight, 1, 2), jnp.swapaxes(up_weight, 1, 2)
    chosen = [
        jnp.dot(picks[e].reshape(-1, row_count), residual, preferred_element_type=f32)
        .astype(bf16)
        .reshape(wide_count, expert_rows, feature_share)
        for e in range(experts_here)
    ]
    arrived = []
    for e in range(experts_here):
        arrived.append(exchange(after(chosen[e], *arrived[-1:])))
    normed_two = [normed_rows(got, mlp_gain_row) for got in arrived]
    row_weights = [weights_of(e, normed_two[e]) for e in range(experts_here)]
    pieces = [gather_pieces(rows) for rows in normed_two]
    waiting = []
    sums = []
    for e in range(experts_here):
        tokens = [after(pieces[e][0], *waiting)] + pieces[e][1:]
        keep, far_rows = expert_partial(
            tokens, gate_rows, up_rows, down_weight, e * parts_here, parts_here
        )
        own, other = split_rows(start_narrow_sum(keep, far_rows))
        waiting = [other]
        sums.append((own, other))
    own_rows = [finish(*sums[e], narrow_count // 2) for e in range(experts_here)]
    back = exchange(cut_rows(own_rows, [w[:, None] for w in row_weights], wide_count))
    mixture = lax.dot_general(
        picks.transpose(1, 0, 2, 3).reshape(-1, row_count),
        back.reshape(-1, feature_share),
        (((0,), (0,)), ((), ())),
        preferred_element_type=f32,
    )
    return (residual.astype(f32) + mixture).astype(bf16)


def solution(mesh):
    placed = (
        P("narrow", "wide"),
        P(),
        P(None, "wide"),
        P("wide", None),
        P("wide", None),
        P("wide", None),
        P(),
        P(),
        P(),
        P(),
        P("narrow", None),
        P("wide", None, "narrow"),
        P("wide", None, "narrow"),
        P("wide", "narrow", None),
    )


    return jax.shard_map(
        body, mesh=mesh, in_specs=placed, out_specs=P("narrow", "wide"), check_vma=False
    )
```
